32 devices in a mesh: ia: 4 (over z), ja: 4 (over y, x), ka: 2 (over core).
Axes of the slice: x: 2, y: 2, z: 4, core: 2. Of those that a mesh axis runs over, the one named last changes fastest.
Arguments:
- blocks: bfloat16 [4, 4, 4, 128, 128, 128], P('ia', 'ja', 'ka'), may hold values from -6 to 6
- coordinates: int32 [3, 4, 4, 4], P(None, 'ia', 'ja', 'ka'), may hold values from 0 to 3, as said below
- occupancy: int32 [4, 4, 4], P('ia', 'ja', 'ka'), may hold values from 0 to 1, as said below
- second_factor: bfloat16 [4, 512, 1024], P('ja', ('ia', 'ka')), may hold values from -12 to 12
- third_factor: bfloat16 [2, 512, 1024], P('ka', ('ia', 'ja')), may hold values from -0.0234375 to 0.0234375
- inverse_first: bfloat16 [1024, 1024], replicated
- inverse_second: bfloat16 [1024, 1024], replicated
Outputs:
- first_new: bfloat16 [4, 512, 1024], P('ia', ('ja', 'ka'))
- second_new: bfloat16 [4, 512, 1024], P('ja', ('ia', 'ka'))
The draws below stay inside these ranges and needn't reach their ends.
Inputs may be any that keep to these rules, and one draw needn't show every extreme that they name: `occupancy`: each device has two slots; its second slot is occupied only where its first is. A device with two blocks is followed along ka, cyclically, by a device with none. Some device holds two blocks. coordinates[0], [1], [2] of a slot are a block row among 4, a block row among 4 and a block layer among 4 of its device's ranges; the two slots of a device name different layers.
All inputs are finite; a program needn't handle non-finite values.
Results may differ from the reference program's by a relative error of at most 0.006.
Values may be sent and summed in bfloat16 or wider, within the bound.
A program may use at most 128 MiB of HBM per device.

```python
import jax
import jax.numpy as jnp
from jax import lax

R = 1024
BLK = 128
SLOTS = 2
IB = 4
JB = 4
KB = 4
N_IA = 4
N_JA = 4
N_KA = 2


def draw_occupancy(key, part):
    subkeys = jax.random.split(jax.random.fold_in(key, 31), 3)
    cycles = N_IA * N_JA
    draws_raw = jax.random.randint(subkeys[0], (cycles, N_KA), 0, 20)
    counts = jnp.where(draws_raw < 7, 0, jnp.where(draws_raw < 14, 1, 2))
    forced_cycle = jax.random.randint(subkeys[1], (), 0, cycles)
    forced_place = jax.random.randint(subkeys[2], (), 0, N_KA)
    cycle_ids = jnp.arange(cycles)[:, None]
    positions = jnp.arange(N_KA)[None, :]
    counts = jnp.where((cycle_ids == forced_cycle) & (positions == forced_place), 2, counts)
    counts = jnp.where((cycle_ids == forced_cycle) & (positions == (forced_place + N_KA - 1) % N_KA), 0, counts)
    previous = jnp.roll(counts, 1, axis=1)
    counts = jnp.where(previous == 2, 0, counts)
    occupied = jnp.stack([counts >= 1, counts >= 2], axis=-1).astype(jnp.int32)
    return occupied.reshape(N_IA, N_JA, N_KA * SLOTS)


def draw_coordinates(key, part):
    subkeys = jax.random.split(jax.random.fold_in(key, 41), 4)
    shape_dev = (N_IA, N_JA, N_KA, SLOTS)
    first_rows = jax.random.randint(subkeys[0], shape_dev, 0, IB)
    second_rows = jax.random.randint(subkeys[1], shape_dev, 0, JB)
    layer_first = jax.random.randint(subkeys[2], (N_IA, N_JA, N_KA), 0, KB)
    layer_step = jax.random.randint(subkeys[3], (N_IA, N_JA, N_KA), 1, KB)
    layers = jnp.stack([layer_first, (layer_first + layer_step) % KB], axis=-1)
    stacked = jnp.stack([first_rows, second_rows, layers], axis=0)
    return stacked.reshape(3, N_IA, N_JA, N_KA * SLOTS).astype(jnp.int32)


def gram_inverse(noise, diag_key):
    diagonal = jax.random.uniform(diag_key, (R,), jnp.float32, 0.4, 1.0)
    symmetric = (noise + noise.T) * (0.2 / (2.0 * R) ** 0.5)
    on_diagonal = jnp.arange(R)[:, None] == jnp.arange(R)[None, :]
    return symmetric + jnp.where(on_diagonal, diagonal[None, :], 0.0)


def draw_inverse_first(key, part):
    subkeys = jax.random.split(jax.random.fold_in(key, 11), 2)
    noise = jax.random.normal(subkeys[0], (R, R), jnp.float32)
    return gram_inverse(noise, subkeys[1]).astype(jnp.bfloat16)


def draw_inverse_second(key, part):
    subkeys = jax.random.split(jax.random.fold_in(key, 12), 2)
    noise = jax.random.normal(subkeys[0], (R, R), jnp.float32)
    return gram_inverse(noise, subkeys[1]).astype(jnp.bfloat16)


def shard_levels(key, extent, pieces, least, largest):
    gain, own = 1.0, jax.random.fold_in(key, 6)
    for dim, shards_of in pieces:
        draws = jnp.exp(jax.random.uniform(jax.random.fold_in(own, dim), (shards_of,), jnp.float32, least / len(pieces), largest / len(pieces)))
        gain = gain * jnp.repeat(draws, extent[dim] // shards_of).reshape([-1 if axis == dim else 1 for axis in range(len(extent))])
    return gain


def gaussian(rng, extent, width, most, cuts=(), kind=jnp.bfloat16):
    drawn = width * jax.random.normal(rng, extent, jnp.float32)
    if cuts:
        drawn = drawn * shard_levels(rng, extent, cuts, -0.22, 0.18)
    return jnp.clip(drawn, -most, most).astype(kind)


def setup_inputs(seed: int = 0) -> dict:
    keys = jax.random.split(jax.random.key(seed), 8)
    return {
        "blocks": gaussian(keys[0], (N_IA, N_JA, N_KA * SLOTS, BLK, BLK, BLK), 1.0, 6.0, ((0, 4), (1, 4), (2, 2))),
        "coordinates": draw_coordinates(jax.random.fold_in(keys[7], 71), 0),
        "occupancy": draw_occupancy(jax.random.fold_in(keys[7], 71), 0),
        "second_factor": gaussian(keys[3], (N_JA, JB * BLK, R), 2.0, 12.0, ((0, 4), (1, 8))),
        "third_factor": gaussian(keys[4], (N_KA, KB * BLK, R), 0.004, 0.0234375, ((0, 2), (1, 16))),
        "inverse_first": draw_inverse_first(jax.random.fold_in(keys[7], 71), 0),
        "inverse_second": draw_inverse_second(jax.random.fold_in(keys[7], 71), 0),
    }


def reference(blocks, coordinates, occupancy, second_factor, third_factor, inverse_first, inverse_second):
    total_slots = N_IA * N_JA * N_KA * SLOTS
    flat_blocks = blocks.reshape(total_slots, BLK, BLK, BLK)
    places = coordinates.reshape(3, total_slots)
    occupied = occupancy.reshape(total_slots)
    slot_ids = jnp.arange(total_slots, dtype=jnp.int32)
    first_plane = slot_ids // (N_JA * N_KA * SLOTS)
    second_plane = (slot_ids // (N_KA * SLOTS)) % N_JA
    third_plane = (slot_ids // SLOTS) % N_KA
    row_block = (first_plane * IB + places[0]).astype(jnp.int32)
    col_block = (second_plane * JB + places[1]).astype(jnp.int32)
    layer_block = (third_plane * KB + places[2]).astype(jnp.int32)
    second_table = second_factor.reshape(N_JA * JB * BLK, R)
    third_table = third_factor.reshape(N_KA * KB * BLK, R)

    def mode_sum(target_rows, own_block, left_block, left_table, swapped):
        def add_block(totals, slot_index):
            def include(carry):
                tensor_block = lax.dynamic_index_in_dim(flat_blocks, slot_index, 0, keepdims=False)
                if swapped:
                    tensor_block = jnp.transpose(tensor_block, (1, 0, 2))
                left_slab = lax.dynamic_slice_in_dim(left_table, left_block[slot_index] * BLK, BLK, 0)
                layer_slab = lax.dynamic_slice_in_dim(third_table, layer_block[slot_index] * BLK, BLK, 0)
                khatri = (left_slab[:, None, :].astype(jnp.float32) * layer_slab[None, :, :].astype(jnp.float32)).astype(jnp.bfloat16)
                product = jnp.dot(tensor_block.reshape(BLK, BLK * BLK), khatri.reshape(BLK * BLK, R), preferred_element_type=jnp.float32)
                row_start = own_block[slot_index] * BLK
                current = lax.dynamic_slice_in_dim(carry, row_start, BLK, 0)
                return lax.dynamic_update_slice_in_dim(carry, current + product, row_start, 0)
            return lax.cond(occupied[slot_index] > 0, include, lambda carry: carry, totals), None
        zeroed = jnp.zeros((target_rows, R), jnp.float32)
        result, unused = lax.scan(add_block, zeroed, slot_ids)
        return result

    first_sum = mode_sum(N_IA * IB * BLK, row_block, col_block, second_table, False)
    first_new = jnp.dot(first_sum.astype(jnp.bfloat16), inverse_first, preferred_element_type=jnp.float32).astype(jnp.bfloat16)
    second_sum = mode_sum(N_JA * JB * BLK, col_block, row_block, first_new, True)
    second_new = jnp.dot(second_sum.astype(jnp.bfloat16), inverse_second, preferred_element_type=jnp.float32).astype(jnp.bfloat16)
    return first_new.reshape(N_IA, IB * BLK, R), second_new.reshape(N_JA, JB * BLK, R)
```

```python
import functools

import jax
import jax.numpy as jnp
from jax import lax
from jax.experimental import pallas as pl
from jax.experimental.pallas import tpu as pltpu
from jax.sharding import PartitionSpec as P

IB = 4
JB = 4
TILES = 4
MESH = pl.DeviceIdType.MESH
AXES = ("ia", "ja", "ka")


def kernel(
    sizes,
    blocks,
    places,
    occupied,
    second_in,
    third_in,
    inverse_first,
    inverse_second,
    first_out,
    second_out,
    xbuf,
    inv1,
    inv2,
    meta_s,
    meta_r,
    cbuf,
    bbuf,
    slab_s,
    slab_r,
    cuse,
    buse,
    tbuf,
    oacc,
    d1s,
    d1r,
    keep1,
    p1s,
    p1r,
    own1,
    fr1,
    abuf,
    d2s,
    d2r,
    keep2,
    p2s,
    p2r,
    own2,
    fr2,
    local_sem,
    once_send,
    once_recv,
    z_send,
    z_recv,
    y_send,
    y_recv,
    k_send,
    k_recv,
):
    na, nb, nc = sizes
    tiles, edge, width = slab_s.shape
    rs, rt = bbuf.shape[3], cbuf.shape[3]
    sh1, sh2 = abuf.shape[3], own2.shape[1]
    a, b, c = (lax.axis_index(name) for name in AXES)
    sent = []

    def away(axis, d):
        n = sizes[AXES.index(axis)]
        me = (a, b, c)[AXES.index(axis)]
        return lax.rem(me + d, n)

    def send(src, dst, send_sem, recv_sem, axis, d):
        copy = pltpu.make_async_remote_copy(
            src_ref=src,
            dst_ref=dst,
            send_sem=send_sem,
            recv_sem=recv_sem,
            device_id={axis: away(axis, d)},
            device_id_type=MESH,
        )
        copy.start()
        sent.append(copy)
        return copy

    def cols(t):
        return pl.ds(t * width, width)

    local = []

    def local_copy(src, dst):
        copy = pltpu.make_async_copy(src, dst, local_sem.at[len(local)])
        copy.start()
        local.append(copy)
        return copy

    own_third = [
        local_copy(third_in.at[0, :, cols(t)], cbuf.at[t, a, b]) for t in range(tiles)
    ]
    own_second = [
        local_copy(second_in.at[0, :, cols(t)], bbuf.at[t, a, c]) for t in range(tiles)
    ]
    own_block = local_copy(blocks.at[0, 0, 0], xbuf.at[0])
    got_inv1 = local_copy(inverse_first, inv1)
    got_inv2 = local_copy(inverse_second, inv2)

    barrier = pltpu.get_barrier_semaphore()
    for axis, n in zip(AXES, sizes):
        for d in range(1, n):
            pl.semaphore_signal(
                barrier, inc=1, device_id={axis: away(axis, d)}, device_id_type=MESH
            )
    keep = occupied[0, 0, 0] > 0
    row0, col0, layer0 = (places[m, 0, 0, 0] for m in range(3))
    row1, col1, layer1 = (places[m, 0, 0, 1] for m in range(3))
    weight1 = jnp.where(occupied[0, 0, 1] > 0, 1.0, 0.0).astype(jnp.float32)
    for q in range(IB):
        value = jnp.where(row1 == q, weight1, 0.0)
        meta_s[pl.ds(q, 1), :] = jnp.full((1, width), value, jnp.float32)
    for q in range(JB):
        value = jnp.where(col1 == q, weight1, 0.0)
        meta_s[pl.ds(IB + q, 1), :] = jnp.full((1, width), value, jnp.float32)
    pl.semaphore_wait(barrier, (na - 1) + (nb - 1) + (nc - 1))

    def chosen(own_value, row):
        own = jnp.where(own_value, 1.0, 0.0).astype(jnp.float32)
        return jnp.where(keep, jnp.full((1, width), own, jnp.float32), meta_r[pl.ds(row, 1), :]) > 0.5

    def third_column(t):
        return [
            send(
                third_in.at[0, :, cols(t)],
                cbuf.at[t, a, b],
                z_send.at[0, t, d - 1],
                z_recv.at[0, t, d - 1],
                "ia",
                d,
            )
            for d in range(1, na)
        ]

    def second_column(t):
        return [
            send(
                second_in.at[0, :, cols(t)],
                bbuf.at[t, a, c],
                z_send.at[1, t, d - 1],
                z_recv.at[1, t, d - 1],
                "ia",
                d,
            )
            for d in range(1, na)
        ]

    third_z, second_z = {}, {}
    third_z[0] = third_column(0)
    block_copy = send(blocks.at[0, 0, 1], xbuf.at[1], once_send.at[0], once_recv.at[0], "ka", 1)
    meta_copy = send(meta_s, meta_r, once_send.at[1], once_recv.at[1], "ka", 1)
    for t in range(1, tiles):
        third_z[t] = third_column(t)
        second_z[t - 1] = second_column(t - 1)
    second_z[tiles - 1] = second_column(tiles - 1)

    third_y, second_k, slab_copy = {}, {}, {}

    def spread_third(t):
        own_third[t].wait()
        for copy in third_z[t]:
            copy.wait_recv()
        third_y[t] = [
            send(
                cbuf.at[t, :, b],
                cbuf.at[t, :, b],
                y_send.at[0, t, d - 1],
                y_recv.at[0, t, d - 1],
                "ja",
                d,
            )
            for d in range(1, nb)
        ]

    def spread_second(t):
        own_second[t].wait()
        for copy in second_z[t]:
            copy.wait_recv()
        second_k[t] = [
            send(
                bbuf.at[t, :, c],
                bbuf.at[t, :, c],
                k_send.at[0, t, d - 1],
                k_recv.at[0, t, d - 1],
                "ka",
                d,
            )
            for d in range(1, nc)
        ]

    def layer_piece(t, layer, piece):
        per = edge // rt
        total = na * nb * rt // edge
        value = None
        for q in range(total):
            s = q * per + piece
            rows = cbuf[t, s // nb, s % nb]
            value = rows if value is None else jnp.where(layer == q, rows, value)
        return value

    def pass_slab(t):
        for copy in third_y[t]:
            copy.wait_recv()
        for piece in range(edge // rt):
            slab_s[t, pl.ds(piece * rt, rt), :] = layer_piece(t, layer1, piece)
        slab_copy[t] = send(
            slab_s.at[t], slab_r.at[t], k_send.at[1, t, 0], k_recv.at[1, t, 0], "ka", 1
        )
        for piece in range(edge // rt):
            cuse[pl.ds(piece * rt, rt), :] = layer_piece(t, layer0, piece)

    def first_products(t):
        for copy in second_k[t]:
            copy.wait_recv()
        if t == 0:
            own_block.wait()
            block_copy.wait_recv()
            meta_copy.wait_recv()
        masks = [chosen(col0 == q, IB + q) for q in range(JB)]
        per = edge // rs
        for piece in range(per):
            value = jnp.zeros((rs, width), jnp.float32)
            for q in range(JB):
                s = q * per + piece
                rows = bbuf[t, s // nc, s % nc].astype(jnp.float32)
                value = jnp.where(masks[q], rows, value)
            buse[pl.ds(piece * rs, rs), :] = value
        slab_copy[t].wait_recv()
        cuse[...] = jnp.where(keep, cuse[...], slab_r[t])
        slot = jnp.where(keep, 0, 1)

        def eight(step, carry):
            base = pl.multiple_of(step * 8, 8)
            sums = []
            for u in range(8):
                product = jnp.dot(
                    xbuf[slot, base + u], cuse[...], preferred_element_type=jnp.float32
                )
                tbuf[t, base + u] = product.astype(jnp.bfloat16)
                sums.append(jnp.sum(product * buse[...], axis=0, keepdims=True))
            oacc[pl.ds(base, 8), :] = jnp.concatenate(sums, axis=0)
            return carry

        lax.fori_loop(0, edge // 8, eight, 0)

    def owned_piece(owner, rows, own_place, meta_row):
        start = owner * rows
        block = start // edge
        off = pl.multiple_of(start % edge, rows)
        mask = chosen(own_place == block, meta_row + block)
        return jnp.where(mask, oacc[pl.ds(off, rows), :], 0.0)

    def pair_sums(t, n, rows, own_place, meta_row, outgoing, arriving, kept, kind):
        copies = []
        for d in range(1, nc):
            for m in range(n):
                owner = m * nc + away("ka", d)
                outgoing[t, d - 1, m] = owned_piece(owner, rows, own_place, meta_row).astype(
                    jnp.bfloat16
                )
            copies.append(
                send(
                    outgoing.at[t, d - 1],
                    arriving.at[t, d - 1],
                    k_send.at[kind, t, d - 1],
                    k_recv.at[kind, t, d - 1],
                    "ka",
                    d,
                )
            )
        for m in range(n):
            kept[t, m] = owned_piece(m * nc + c, rows, own_place, meta_row)
        return copies

    def chip_sums(t, axis, n, copies, arriving, kept, outgoing, landing, own, sends, recvs, kind):
        for copy in copies:
            copy.wait_recv()
        started = []
        for d in range(n):
            m = away(axis, d)
            value = kept[t, m]
            for e in range(1, nc):
                value = value + arriving[t, e - 1, m].astype(jnp.float32)
            if d == 0:
                own[t] = value
            else:
                outgoing[t, d - 1] = value.astype(jnp.bfloat16)
                started.append(
                    send(
                        outgoing.at[t, d - 1],
                        landing.at[t, d - 1],
                        sends.at[kind, t, d - 1],
                        recvs.at[kind, t, d - 1],
                        axis,
                        d,
                    )
                )
        return started

    first_k, first_y = {}, {}

    def first_chip_sums(t):
        first_y[t] = chip_sums(
            t, "ja", nb, first_k[t], d1r, keep1, p1s, p1r, own1, y_send, y_recv, 1
        )

    spread_third(0)
    spread_second(0)
    for t in range(tiles):
        if t + 1 < tiles:
            spread_third(t + 1)
        pass_slab(t)
        if t:
            first_chip_sums(t - 1)
        first_products(t)
        first_k[t] = pair_sums(t, nb, sh1, row0, 0, d1s, d1r, keep1, 2)
        if t + 1 < tiles:
            spread_second(t + 1)
    first_chip_sums(tiles - 1)

    def gathered(t, copies, own, landing, n):
        for copy in copies:
            copy.wait_recv()
        value = own[t]
        for d in range(1, n):
            value = value + landing[t, d - 1].astype(jnp.float32)
        return value.astype(jnp.bfloat16)

    for t in range(tiles):
        fr1[:, cols(t)] = gathered(t, first_y[t], own1, p1r, nb)
    got_inv1.wait()
    new_y, new_k = {}, {}
    for t in range(tiles):
        value = jnp.dot(fr1[...], inv1[:, cols(t)], preferred_element_type=jnp.float32)
        value = value.astype(jnp.bfloat16)
        abuf[t, b, c] = value
        first_out[0, :, cols(t)] = value
        new_y[t] = [
            send(
                abuf.at[t, b, c],
                abuf.at[t, b, c],
                y_send.at[2, t, d - 1],
                y_recv.at[2, t, d - 1],
                "ja",
                d,
            )
            for d in range(1, nb)
        ]

    def spread_new(t):
        for copy in new_y[t]:
            copy.wait_recv()
        new_k[t] = [
            send(
                abuf.at[t, :, c],
                abuf.at[t, :, c],
                k_send.at[3, t, d - 1],
                k_recv.at[3, t, d - 1],
                "ka",
                d,
            )
            for d in range(1, nc)
        ]

    def second_products(t):
        for copy in new_k[t]:
            copy.wait_recv()
        masks = [chosen(row0 == q, q) for q in range(IB)]
        per = edge // sh1
        for piece in range(per):
            value = jnp.zeros((sh1, width), jnp.float32)
            for q in range(IB):
                s = q * per + piece
                rows = abuf[t, s // nc, s % nc].astype(jnp.float32)
                value = jnp.where(masks[q], rows, value)
            buse[pl.ds(piece * sh1, sh1), :] = value
        lanes = 128
        for lane in range(0, width, lanes):

            def eight(step, total):
                base = pl.multiple_of(step * 8, 8)
                rows = buse[pl.ds(base, 8), pl.ds(lane, lanes)]
                for u in range(8):
                    total = total + rows[u : u + 1] * tbuf[t, base + u, :, pl.ds(lane, lanes)].astype(
                        jnp.float32
                    )
                return total

            oacc[:, pl.ds(lane, lanes)] = lax.fori_loop(
                0, edge // 8, eight, jnp.zeros((edge, lanes), jnp.float32)
            )

    second_s, second_y = {}, {}

    def second_chip_sums(t):
        second_y[t] = chip_sums(
            t, "ia", na, second_s[t], d2r, keep2, p2s, p2r, own2, z_send, z_recv, 2
        )

    spread_new(0)
    for t in range(tiles):
        if t + 1 < tiles:
            spread_new(t + 1)
        second_products(t)
        second_s[t] = pair_sums(t, na, sh2, col0, IB, d2s, d2r, keep2, 4)
        if t:
            second_chip_sums(t - 1)
    second_chip_sums(tiles - 1)
    for t in range(tiles):
        fr2[:, cols(t)] = gathered(t, second_y[t], own2, p2r, na)
    got_inv2.wait()
    for t in range(tiles):
        value = jnp.dot(fr2[...], inv2[:, cols(t)], preferred_element_type=jnp.float32)
        second_out[0, :, cols(t)] = value.astype(jnp.bfloat16)
    for copy in sent:
        copy.wait_send()


def body(
    sizes,
    blocks,
    coordinates,
    occupancy,
    second_factor,
    third_factor,
    inverse_first,
    inverse_second,
):
    na, nb, nc = sizes
    edge, rank = blocks.shape[-1], inverse_first.shape[0]
    tiles = TILES
    width = rank // tiles
    rs, rt = second_factor.shape[1], third_factor.shape[1]
    sh1, sh2 = IB * edge // (nb * nc), JB * edge // (na * nc)
    bf16, f32 = jnp.bfloat16, jnp.float32
    dma = pltpu.SemaphoreType.DMA
    widest_k = max(nc - 1, 1)
    vmem = pl.BlockSpec(memory_space=pltpu.VMEM)
    smem = pl.BlockSpec(memory_space=pltpu.SMEM)
    anywhere = pl.BlockSpec(memory_space=pl.ANY)
    scratch = [
        pltpu.VMEM((2, edge, edge, edge), bf16),
        pltpu.VMEM((rank, rank), bf16),
        pltpu.VMEM((rank, rank), bf16),
        pltpu.VMEM((IB + JB, width), f32),
        pltpu.VMEM((IB + JB, width), f32),
        pltpu.VMEM((tiles, na, nb, rt, width), bf16),
        pltpu.VMEM((tiles, na, nc, rs, width), bf16),
        pltpu.VMEM((tiles, edge, width), bf16),
        pltpu.VMEM((tiles, edge, width), bf16),
        pltpu.VMEM((edge, width), bf16),
        pltpu.VMEM((edge, width), f32),
        pltpu.VMEM((tiles, edge, edge, width), bf16),
        pltpu.VMEM((edge, width), f32),
        pltpu.VMEM((tiles, nc - 1, nb, sh1, width), bf16),
        pltpu.VMEM((tiles, nc - 1, nb, sh1, width), bf16),
        pltpu.VMEM((tiles, nb, sh1, width), f32),
        pltpu.VMEM((tiles, nb - 1, sh1, width), bf16),
        pltpu.VMEM((tiles, nb - 1, sh1, width), bf16),
        pltpu.VMEM((tiles, sh1, width), f32),
        pltpu.VMEM((sh1, rank), bf16),
        pltpu.VMEM((tiles, nb, nc, sh1, width), bf16),
        pltpu.VMEM((tiles, nc - 1, na, sh2, width), bf16),
        pltpu.VMEM((tiles, nc - 1, na, sh2, width), bf16),
        pltpu.VMEM((tiles, na, sh2, width), f32),
        pltpu.VMEM((tiles, na - 1, sh2, width), bf16),
        pltpu.VMEM((tiles, na - 1, sh2, width), bf16),
        pltpu.VMEM((tiles, sh2, width), f32),
        pltpu.VMEM((sh2, rank), bf16),
        dma((2 * tiles + 3,)),
        dma((2,)),
        dma((2,)),
        dma((3, tiles, na - 1)),
        dma((3, tiles, na - 1)),
        dma((3, tiles, nb - 1)),
        dma((3, tiles, nb - 1)),
        dma((5, tiles, widest_k)),
        dma((5, tiles, widest_k)),
    ]
    return pl.pallas_call(
        functools.partial(kernel, sizes),
        name="als",
        out_shape=(
            jax.ShapeDtypeStruct((1, sh1, rank), bf16),
            jax.ShapeDtypeStruct((1, sh2, rank), bf16),
        ),
        in_specs=[anywhere, smem, smem, vmem, vmem, anywhere, anywhere],
        out_specs=(vmem, vmem),
        scratch_shapes=scratch,
        compiler_params=pltpu.CompilerParams(
            collective_id=0, has_side_effects=True, vmem_limit_bytes=67043328
        ),
    )(blocks, coordinates, occupancy, second_factor, third_factor, inverse_first, inverse_second)


def solution(mesh):
    sizes = tuple(mesh.shape[name] for name in AXES)
    in_specs = (
        P("ia", "ja", "ka", None, None, None),
        P(None, "ia", "ja", "ka"),
        P("ia", "ja", "ka"),
        P("ja", ("ia", "ka"), None),
        P("ka", ("ia", "ja"), None),
        P(),
        P(),
    )
    out_specs = (P("ia", ("ja", "ka"), None), P("ja", ("ia", "ka"), None))
    return jax.shard_map(
        functools.partial(body, sizes),
        mesh=mesh,
        in_specs=in_specs,
        out_specs=out_specs,
        check_vma=False,
    )
```

```python
import functools

import jax
import jax.numpy as jnp
from jax import lax
from jax.experimental import pallas as pl
from jax.experimental.pallas import tpu as pltpu
from jax.sharding import PartitionSpec as P

IB = 4
JB = 4
TILES = 4
MESH = pl.DeviceIdType.MESH
AXES = ("ia", "ja", "ka")


def kernel(
    sizes,
    blocks,
    places_in,
    occupied_in,
    second_in,
    third_in,
    inverse_first,
    inverse_second,
    first_out,
    second_out,
    xbuf,
    inv1,
    inv2,
    meta_s,
    meta_r,
    cbuf,
    bbuf,
    slab_s,
    slab_r,
    cuse,
    buse,
    tbuf,
    oacc,
    d1s,
    d1r,
    keep1,
    p1s,
    p1r,
    own1,
    fr1,
    abuf,
    d2s,
    d2r,
    keep2,
    p2s,
    p2r,
    own2,
    fr2,
    places,
    occupied,
    local_sem,
    once_send,
    once_recv,
    z_send,
    z_recv,
    y_send,
    y_recv,
    k_send,
    k_recv,
):
    na, nb, nc = sizes
    tiles, edge, width = slab_s.shape
    rs, rt = bbuf.shape[3], cbuf.shape[3]
    sh1, sh2 = abuf.shape[3], own2.shape[1]
    a, b, c = (lax.axis_index(name) for name in AXES)
    sent = []

    def away(axis, d):
        n = sizes[AXES.index(axis)]
        me = (a, b, c)[AXES.index(axis)]
        return lax.rem(me + d, n)

    def send(src, dst, send_sem, recv_sem, axis, d):
        copy = pltpu.make_async_remote_copy(
            src_ref=src,
            dst_ref=dst,
            send_sem=send_sem,
            recv_sem=recv_sem,
            device_id={axis: away(axis, d)},
            device_id_type=MESH,
        )
        copy.start()
        sent.append(copy)
        return copy

    def cols(t):
        return pl.ds(t * width, width)

    local = []

    def local_copy(src, dst):
        copy = pltpu.make_async_copy(src, dst, local_sem.at[len(local)])
        copy.start()
        local.append(copy)
        return copy

    got_places = local_copy(places_in, places)
    got_occupied = local_copy(occupied_in, occupied)
    own_third = [
        local_copy(third_in.at[0, :, cols(t)], cbuf.at[t, a, b]) for t in range(tiles)
    ]
    own_second = [
        local_copy(second_in.at[0, :, cols(t)], bbuf.at[t, a, c]) for t in range(tiles)
    ]
    own_block = local_copy(blocks.at[0, 0, 0], xbuf.at[0])
    got_inv1 = local_copy(inverse_first, inv1)
    got_inv2 = local_copy(inverse_second, inv2)

    barrier = pltpu.get_barrier_semaphore()
    for axis, n in zip(AXES, sizes):
        for d in range(1, n):
            pl.semaphore_signal(
                barrier, inc=1, device_id={axis: away(axis, d)}, device_id_type=MESH
            )
    got_places.wait()
    got_occupied.wait()
    keep = occupied[0, 0, 0] > 0
    row0, col0, layer0 = (places[m, 0, 0, 0] for m in range(3))
    row1, col1, layer1 = (places[m, 0, 0, 1] for m in range(3))
    weight1 = jnp.where(occupied[0, 0, 1] > 0, 1.0, 0.0).astype(jnp.float32)
    for q in range(IB):
        value = jnp.where(row1 == q, weight1, 0.0)
        meta_s[pl.ds(q, 1), :] = jnp.full((1, width), value, jnp.float32)
    for q in range(JB):
        value = jnp.where(col1 == q, weight1, 0.0)
        meta_s[pl.ds(IB + q, 1), :] = jnp.full((1, width), value, jnp.float32)
    pl.semaphore_wait(barrier, (na - 1) + (nb - 1) + (nc - 1))

    def chosen(own_value, row):
        own = jnp.where(own_value, 1.0, 0.0).astype(jnp.float32)
        return jnp.where(keep, jnp.full((1, width), own, jnp.float32), meta_r[pl.ds(row, 1), :]) > 0.5

    def third_column(t):
        return [
            send(
                third_in.at[0, :, cols(t)],
                cbuf.at[t, a, b],
                z_send.at[0, t, d - 1],
                z_recv.at[0, t, d - 1],
                "ia",
                d,
            )
            for d in range(1, na)
        ]

    def second_column(t):
        return [
            send(
                second_in.at[0, :, cols(t)],
                bbuf.at[t, a, c],
                z_send.at[1, t, d - 1],
                z_recv.at[1, t, d - 1],
                "ia",
                d,
            )
            for d in range(1, na)
        ]

    third_z, second_z = {}, {}
    third_z[0] = third_column(0)
    block_copy = send(blocks.at[0, 0, 1], xbuf.at[1], once_send.at[0], once_recv.at[0], "ka", 1)
    meta_copy = send(meta_s, meta_r, once_send.at[1], once_recv.at[1], "ka", 1)
    for t in range(1, tiles):
        third_z[t] = third_column(t)
        second_z[t - 1] = second_column(t - 1)
    second_z[tiles - 1] = second_column(tiles - 1)

    third_y, second_k, slab_copy = {}, {}, {}

    def spread_third(t):
        own_third[t].wait()
        for copy in third_z[t]:
            copy.wait_recv()
        third_y[t] = [
            send(
                cbuf.at[t, :, b],
                cbuf.at[t, :, b],
                y_send.at[0, t, d - 1],
                y_recv.at[0, t, d - 1],
                "ja",
                d,
            )
            for d in range(1, nb)
        ]

    def spread_second(t):
        own_second[t].wait()
        for copy in second_z[t]:
            copy.wait_recv()
        second_k[t] = [
            send(
                bbuf.at[t, :, c],
                bbuf.at[t, :, c],
                k_send.at[0, t, d - 1],
                k_recv.at[0, t, d - 1],
                "ka",
                d,
            )
            for d in range(1, nc)
        ]

    def layer_piece(t, layer, piece):
        per = edge // rt
        total = na * nb * rt // edge
        value = None
        for q in range(total):
            s = q * per + piece
            rows = cbuf[t, s // nb, s % nb]
            value = rows if value is None else jnp.where(layer == q, rows, value)
        return value

    def pass_slab(t):
        for copy in third_y[t]:
            copy.wait_recv()
        for piece in range(edge // rt):
            slab_s[t, pl.ds(piece * rt, rt), :] = layer_piece(t, layer1, piece)
        slab_copy[t] = send(
            slab_s.at[t], slab_r.at[t], k_send.at[1, t, 0], k_recv.at[1, t, 0], "ka", 1
        )
        for piece in range(edge // rt):
            cuse[pl.ds(piece * rt, rt), :] = layer_piece(t, layer0, piece)

    def first_products(t):
        for copy in second_k[t]:
            copy.wait_recv()
        if t == 0:
            own_block.wait()
            block_copy.wait_recv()
            meta_copy.wait_recv()
        masks = [chosen(col0 == q, IB + q) for q in range(JB)]
        per = edge // rs
        for piece in range(per):
            value = jnp.zeros((rs, width), jnp.float32)
            for q in range(JB):
                s = q * per + piece
                rows = bbuf[t, s // nc, s % nc].astype(jnp.float32)
                value = jnp.where(masks[q], rows, value)
            buse[pl.ds(piece * rs, rs), :] = value
        slab_copy[t].wait_recv()
        cuse[...] = jnp.where(keep, cuse[...], slab_r[t])
        slot = jnp.where(keep, 0, 1)

        def eight(step, carry):
            base = pl.multiple_of(step * 8, 8)
            sums = []
            for u in range(8):
                product = jnp.dot(
                    xbuf[slot, base + u], cuse[...], preferred_element_type=jnp.float32
                )
                tbuf[t, base + u] = product.astype(jnp.bfloat16)
                sums.append(jnp.sum(product * buse[...], axis=0, keepdims=True))
            oacc[pl.ds(base, 8), :] = jnp.concatenate(sums, axis=0)
            return carry

        lax.fori_loop(0, edge // 8, eight, 0)

    def owned_piece(owner, rows, own_place, meta_row):
        start = owner * rows
        block = start // edge
        off = pl.multiple_of(start % edge, rows)
        mask = chosen(own_place == block, meta_row + block)
        return jnp.where(mask, oacc[pl.ds(off, rows), :], 0.0)

    def pair_sums(t, n, rows, own_place, meta_row, outgoing, arriving, kept, kind):
        copies = []
        for d in range(1, nc):
            for m in range(n):
                owner = m * nc + away("ka", d)
                outgoing[t, d - 1, m] = owned_piece(owner, rows, own_place, meta_row).astype(
                    jnp.bfloat16
                )
            copies.append(
                send(
                    outgoing.at[t, d - 1],
                    arriving.at[t, d - 1],
                    k_send.at[kind, t, d - 1],
                    k_recv.at[kind, t, d - 1],
                    "ka",
                    d,
                )
            )
        for m in range(n):
            kept[t, m] = owned_piece(m * nc + c, rows, own_place, meta_row)
        return copies

    def chip_sums(t, axis, n, copies, arriving, kept, outgoing, landing, own, sends, recvs, kind):
        for copy in copies:
            copy.wait_recv()
        started = []
        for d in range(n):
            m = away(axis, d)
            value = kept[t, m]
            for e in range(1, nc):
                value = value + arriving[t, e - 1, m].astype(jnp.float32)
            if d == 0:
                own[t] = value
            else:
                outgoing[t, d - 1] = value.astype(jnp.bfloat16)
                started.append(
                    send(
                        outgoing.at[t, d - 1],
                        landing.at[t, d - 1],
                        sends.at[kind, t, d - 1],
                        recvs.at[kind, t, d - 1],
                        axis,
                        d,
                    )
                )
        return started

    first_k, first_y = {}, {}

    def first_chip_sums(t):
        first_y[t] = chip_sums(
            t, "ja", nb, first_k[t], d1r, keep1, p1s, p1r, own1, y_send, y_recv, 1
        )

    spread_third(0)
    spread_second(0)
    for t in range(tiles):
        if t + 1 < tiles:
            spread_third(t + 1)
        pass_slab(t)
        if t:
            first_chip_sums(t - 1)
        first_products(t)
        first_k[t] = pair_sums(t, nb, sh1, row0, 0, d1s, d1r, keep1, 2)
        if t + 1 < tiles:
            spread_second(t + 1)
    first_chip_sums(tiles - 1)

    def gathered(t, copies, own, landing, n):
        for copy in copies:
            copy.wait_recv()
        value = own[t]
        for d in range(1, n):
            value = value + landing[t, d - 1].astype(jnp.float32)
        return value.astype(jnp.bfloat16)

    for t in range(tiles):
        fr1[:, cols(t)] = gathered(t, first_y[t], own1, p1r, nb)
    got_inv1.wait()
    new_y, new_k = {}, {}
    for t in range(tiles):
        value = jnp.dot(fr1[...], inv1[:, cols(t)], preferred_element_type=jnp.float32)
        value = value.astype(jnp.bfloat16)
        abuf[t, b, c] = value
        first_out[0, :, cols(t)] = value
        new_y[t] = [
            send(
                abuf.at[t, b, c],
                abuf.at[t, b, c],
                y_send.at[2, t, d - 1],
                y_recv.at[2, t, d - 1],
                "ja",
                d,
            )
            for d in range(1, nb)
        ]

    def spread_new(t):
        for copy in new_y[t]:
            copy.wait_recv()
        new_k[t] = [
            send(
                abuf.at[t, :, c],
                abuf.at[t, :, c],
                k_send.at[3, t, d - 1],
                k_recv.at[3, t, d - 1],
                "ka",
                d,
            )
            for d in range(1, nc)
        ]

    def second_products(t):
        for copy in new_k[t]:
            copy.wait_recv()
        masks = [chosen(row0 == q, q) for q in range(IB)]
        per = edge // sh1
        for piece in range(per):
            value = jnp.zeros((sh1, width), jnp.float32)
            for q in range(IB):
                s = q * per + piece
                rows = abuf[t, s // nc, s % nc].astype(jnp.float32)
                value = jnp.where(masks[q], rows, value)
            buse[pl.ds(piece * sh1, sh1), :] = value
        lanes = 128
        for lane in range(0, width, lanes):

            def eight(step, total):
                base = pl.multiple_of(step * 8, 8)
                rows = buse[pl.ds(base, 8), pl.ds(lane, lanes)]
                for u in range(8):
                    total = total + rows[u : u + 1] * tbuf[t, base + u, :, pl.ds(lane, lanes)].astype(
                        jnp.float32
                    )
                return total

            oacc[:, pl.ds(lane, lanes)] = lax.fori_loop(
                0, edge // 8, eight, jnp.zeros((edge, lanes), jnp.float32)
            )

    second_s, second_y = {}, {}

    def second_chip_sums(t):
        second_y[t] = chip_sums(
            t, "ia", na, second_s[t], d2r, keep2, p2s, p2r, own2, z_send, z_recv, 2
        )

    spread_new(0)
    for t in range(tiles):
        if t + 1 < tiles:
            spread_new(t + 1)
        second_products(t)
        second_s[t] = pair_sums(t, na, sh2, col0, IB, d2s, d2r, keep2, 4)
        if t:
            second_chip_sums(t - 1)
    second_chip_sums(tiles - 1)
    for t in range(tiles):
        fr2[:, cols(t)] = gathered(t, second_y[t], own2, p2r, na)
    got_inv2.wait()
    for t in range(tiles):
        value = jnp.dot(fr2[...], inv2[:, cols(t)], preferred_element_type=jnp.float32)
        second_out[0, :, cols(t)] = value.astype(jnp.bfloat16)
    for copy in sent:
        copy.wait_send()


def body(
    sizes,
    blocks,
    coordinates,
    occupancy,
    second_factor,
    third_factor,
    inverse_first,
    inverse_second,
):
    na, nb, nc = sizes
    edge, rank = blocks.shape[-1], inverse_first.shape[0]
    tiles = TILES
    width = rank // tiles
    rs, rt = second_factor.shape[1], third_factor.shape[1]
    sh1, sh2 = IB * edge // (nb * nc), JB * edge // (na * nc)
    bf16, f32 = jnp.bfloat16, jnp.float32
    dma = pltpu.SemaphoreType.DMA
    widest_k = max(nc - 1, 1)
    vmem = pl.BlockSpec(memory_space=pltpu.VMEM)
    anywhere = pl.BlockSpec(memory_space=pl.ANY)
    scratch = [
        pltpu.VMEM((2, edge, edge, edge), bf16),
        pltpu.VMEM((rank, rank), bf16),
        pltpu.VMEM((rank, rank), bf16),
        pltpu.VMEM((IB + JB, width), f32),
        pltpu.VMEM((IB + JB, width), f32),
        pltpu.VMEM((tiles, na, nb, rt, width), bf16),
        pltpu.VMEM((tiles, na, nc, rs, width), bf16),
        pltpu.VMEM((tiles, edge, width), bf16),
        pltpu.VMEM((tiles, edge, width), bf16),
        pltpu.VMEM((edge, width), bf16),
        pltpu.VMEM((edge, width), f32),
        pltpu.VMEM((tiles, edge, edge, width), bf16),
        pltpu.VMEM((edge, width), f32),
        pltpu.VMEM((tiles, nc - 1, nb, sh1, width), bf16),
        pltpu.VMEM((tiles, nc - 1, nb, sh1, width), bf16),
        pltpu.VMEM((tiles, nb, sh1, width), f32),
        pltpu.VMEM((tiles, nb - 1, sh1, width), bf16),
        pltpu.VMEM((tiles, nb - 1, sh1, width), bf16),
        pltpu.VMEM((tiles, sh1, width), f32),
        pltpu.VMEM((sh1, rank), bf16),
        pltpu.VMEM((tiles, nb, nc, sh1, width), bf16),
        pltpu.VMEM((tiles, nc - 1, na, sh2, width), bf16),
        pltpu.VMEM((tiles, nc - 1, na, sh2, width), bf16),
        pltpu.VMEM((tiles, na, sh2, width), f32),
        pltpu.VMEM((tiles, na - 1, sh2, width), bf16),
        pltpu.VMEM((tiles, na - 1, sh2, width), bf16),
        pltpu.VMEM((tiles, sh2, width), f32),
        pltpu.VMEM((sh2, rank), bf16),
        pltpu.SMEM(coordinates.shape, jnp.int32),
        pltpu.SMEM(occupancy.shape, jnp.int32),
        dma((2 * tiles + 5,)),
        dma((2,)),
        dma((2,)),
        dma((3, tiles, na - 1)),
        dma((3, tiles, na - 1)),
        dma((3, tiles, nb - 1)),
        dma((3, tiles, nb - 1)),
        dma((5, tiles, widest_k)),
        dma((5, tiles, widest_k)),
    ]
    results = pl.pallas_call(
        functools.partial(kernel, sizes),
        name="als",
        out_shape=(
            jax.ShapeDtypeStruct((1, sh1, rank), bf16),
            jax.ShapeDtypeStruct((1, sh2, rank), bf16),
        ),
        in_specs=[anywhere, anywhere, anywhere, vmem, vmem, anywhere, anywhere],
        out_specs=(vmem, vmem),
        scratch_shapes=scratch,
        compiler_params=pltpu.CompilerParams(
            collective_id=0, has_side_effects=True, vmem_limit_bytes=67043328
        ),
    )(blocks, coordinates, occupancy, second_factor, third_factor, inverse_first, inverse_second)
    return pl.pallas_call(
        hand_over,
        name="hand_over",
        out_shape=tuple(jax.ShapeDtypeStruct(x.shape, x.dtype) for x in results),
        in_specs=[vmem, vmem],
        out_specs=(vmem, vmem),
    )(*results)


def hand_over(first_in, second_in, first_out, second_out):
    first_out[...] = first_in[...]
    second_out[...] = second_in[...]


def solution(mesh):
    sizes = tuple(mesh.shape[name] for name in AXES)
    in_specs = (
        P("ia", "ja", "ka", None, None, None),
        P(None, "ia", "ja", "ka"),
        P("ia", "ja", "ka"),
        P("ja", ("ia", "ka"), None),
        P("ka", ("ia", "ja"), None),
        P(),
        P(),
    )
    out_specs = (P("ia", ("ja", "ka"), None), P("ja", ("ia", "ka"), None))
    return jax.shard_map(
        functools.partial(body, sizes),
        mesh=mesh,
        in_specs=in_specs,
        out_specs=out_specs,
        check_vma=False,
    )
```
